512 devices in a mesh: angle: 8 (over x, core), gx: 16 (over y, z_lo), gy: 4 (over z_hi).
Axes of the slice: x: 4, y: 8, z: 8 (z_hi: 4, z_lo: 2; z = z_hi * 2 + z_lo), core: 2. Of those that a mesh axis runs over, the one named last changes fastest.
Arguments:
- forward_fields: float32 [8, 12, 128, 64, 128], P('angle', None, 'gx', 'gy'), may hold values from -6 to 6
- adjoint_fields: float32 [8, 12, 128, 64, 128], P('angle', None, 'gx', 'gy'), may hold values from -6 to 6
- forward_spectrum: float32 [8, 6, 128, 64, 128], P('angle', None, 'gx', 'gy'), may hold values from -6 to 6
- adjoint_spectrum: float32 [8, 6, 128, 64, 128], P('angle', None, 'gx', 'gy'), may hold values from -6 to 6
- permittivity: float32 [128, 64, 128], P('gx', 'gy'), may hold values from 1 to 12
- phase_table: float32 [8, 2], replicated, may hold values from -3.140625 to 3.140625
- angle_index: int32 [8], P('angle'), may hold values from 0 to 7, each once
- design_tiles: int32 [16], replicated, may hold values from 0 to 63, as said below
Outputs:
- forward_transform: float32 [8, 6, 128, 64, 128], P('angle', None, 'gx', 'gy')
- adjoint_transform: float32 [8, 6, 128, 64, 128], P('angle', None, 'gx', 'gy')
- gradient: float32 [128, 64, 128], P('gx', 'gy', 'angle')
The draws below stay inside these ranges and needn't reach their ends.
Inputs may be any that keep to these rules, and one draw needn't show every extreme that they name: `angle_index`: every row of phase_table is used by exactly one angle. `design_tiles`: 16 distinct tile numbers; tiles 0 and 63 are always among them.
All inputs are finite; a program needn't handle non-finite values.
Results may differ from the reference program's by a relative error of at most 0.0001.
Values sent between devices are 32-bit elements; how exact they have to be, the bound alone decides.
A program may use at most 64 MiB of HBM per device.

```python
import math
import jax
import jax.numpy as jnp
from jax import lax

CX = 8
CY = 16
NZ = 128
STEPS = 3
ANGLES = 8
NX = 128
NY = 64
TILES = 64
NDES = 16
N_GY = 4


def draw_design_tiles(key, part):
    others = jax.random.permutation(jax.random.fold_in(key, 7), TILES - 2)[:NDES - 2] + 1
    chosen = jnp.concatenate([jnp.array([0, TILES - 1], dtype=jnp.int32), others.astype(jnp.int32)])
    order = jax.random.permutation(jax.random.fold_in(key, 11), NDES)
    return chosen[order].astype(jnp.int32)


def block_scale(own_key, shape, cuts, least, high):
    level, own = 1.0, jax.random.fold_in(own_key, 6)
    for position, shards_of in cuts:
        draws = jnp.exp(jax.random.uniform(jax.random.fold_in(own, position), (shards_of,), jnp.float32, least / len(cuts), high / len(cuts)))
        level = level * jnp.repeat(draws, shape[position] // shards_of).reshape([-1 if axis == position else 1 for axis in range(len(shape))])
    return level


def bell_draw(stream_key, shape, scale, limit, pieces=(), kind=jnp.bfloat16):
    entries = scale * jax.random.normal(stream_key, shape, jnp.float32)
    if pieces:
        entries = entries * block_scale(stream_key, shape, pieces, -0.22, 0.18)
    return jnp.clip(entries, -limit, limit).astype(kind)


def setup_inputs(seed: int = 0) -> dict:
    streams_of = jax.random.split(jax.random.key(seed), 9)
    return {
        "forward_fields": bell_draw(streams_of[0], (ANGLES, 12, NX, NY, NZ), 1.0, 6.0, ((0, 8), (2, 16), (3, 4)), jnp.float32),
        "adjoint_fields": bell_draw(streams_of[1], (ANGLES, 12, NX, NY, NZ), 1.0, 6.0, ((0, 8), (2, 16), (3, 4)), jnp.float32),
        "forward_spectrum": bell_draw(streams_of[2], (ANGLES, 6, NX, NY, NZ), 1.0, 6.0, ((0, 8), (2, 16), (3, 4)), jnp.float32),
        "adjoint_spectrum": bell_draw(streams_of[3], (ANGLES, 6, NX, NY, NZ), 1.0, 6.0, ((0, 8), (2, 16), (3, 4)), jnp.float32),
        "permittivity": jnp.clip(1.0 + 11.0 * jax.random.uniform(streams_of[4], (NX, NY, NZ), jnp.float32) ** block_scale(streams_of[4], (NX, NY, NZ), ((0, 16), (1, 4)), -0.2, 0.2), 1.0, 12.0),
        "phase_table": jnp.clip(jax.random.uniform(streams_of[5], (ANGLES, 2), jnp.float32, -3.140625, 3.140625), -3.140625, 3.140625),
        "angle_index": jax.random.permutation(streams_of[6], ANGLES).astype(jnp.int32),
        "design_tiles": draw_design_tiles(jax.random.fold_in(streams_of[8], 71), 0),
    }


courant = 0.5
omega_step = 0.7


def rotate_pair(pair, cosine, sine):
    real_part = pair[0]
    imag_part = pair[1]
    return jnp.stack([real_part * cosine - imag_part * sine, real_part * sine + imag_part * cosine])


def next_along(pair, axis, cosine, sine):
    rolled = jnp.roll(pair, -1, axis)
    count = pair.shape[axis]
    edge = lax.broadcasted_iota(jnp.int32, pair.shape, axis) == count - 1
    return jnp.where(edge, rotate_pair(rolled, cosine, sine), rolled)


def prev_along(pair, axis, cosine, sine):
    rolled = jnp.roll(pair, 1, axis)
    edge = lax.broadcasted_iota(jnp.int32, pair.shape, axis) == 0
    return jnp.where(edge, rotate_pair(rolled, cosine, -sine), rolled)


def next_depth(field):
    return jnp.concatenate([field[..., 1:], jnp.zeros_like(field[..., :1])], axis=-1)


def prev_depth(field):
    return jnp.concatenate([jnp.zeros_like(field[..., :1]), field[..., :-1]], axis=-1)


def curl_forward(efield, cos_x, sin_x, cos_y, sin_y):
    comp_x = efield[:, 0]
    comp_y = efield[:, 1]
    comp_z = efield[:, 2]
    dz_dy = next_along(comp_z, 2, cos_y, sin_y) - comp_z
    dy_dz = next_depth(comp_y) - comp_y
    dx_dz = next_depth(comp_x) - comp_x
    dz_dx = next_along(comp_z, 1, cos_x, sin_x) - comp_z
    dy_dx = next_along(comp_y, 1, cos_x, sin_x) - comp_y
    dx_dy = next_along(comp_x, 2, cos_y, sin_y) - comp_x
    return jnp.stack([dz_dy - dy_dz, dx_dz - dz_dx, dy_dx - dx_dy], axis=1)


def curl_backward(hfield, cos_x, sin_x, cos_y, sin_y):
    comp_x = hfield[:, 0]
    comp_y = hfield[:, 1]
    comp_z = hfield[:, 2]
    first = (comp_z - prev_along(comp_z, 2, cos_y, sin_y)) - (comp_y - prev_depth(comp_y))
    second = (comp_x - prev_depth(comp_x)) - (comp_z - prev_along(comp_z, 1, cos_x, sin_x))
    third = (comp_y - prev_along(comp_y, 1, cos_x, sin_x)) - (comp_x - prev_along(comp_x, 2, cos_y, sin_y))
    return jnp.stack([first, second, third], axis=1)


def advance(fields, spectrum, permittivity, cos_x, sin_x, cos_y, sin_y):
    cells = fields.shape[1:]
    efield = fields[0:6].reshape((2, 3) + cells)
    hfield = fields[6:12].reshape((2, 3) + cells)
    spectrum = spectrum.reshape((2, 3) + cells)
    coef = courant / permittivity
    for step in range(STEPS):
        hfield = hfield - courant * curl_forward(efield, cos_x, sin_x, cos_y, sin_y)
        efield = efield + coef * curl_backward(hfield, cos_x, sin_x, cos_y, sin_y)
        theta = omega_step * (step + 1)
        spectrum = spectrum + rotate_pair(efield, math.cos(theta), math.sin(theta))
    return spectrum


def reference(forward_fields, adjoint_fields, forward_spectrum, adjoint_spectrum, permittivity, phase_table, angle_index, design_tiles):
    total = jnp.zeros((NX, NY, NZ), jnp.float32)
    forward_list = []
    adjoint_list = []
    for angle in range(ANGLES):
        row = phase_table[angle_index[angle]]
        cos_x = jnp.cos(row[0])
        sin_x = jnp.sin(row[0])
        cos_y = jnp.cos(row[1])
        sin_y = jnp.sin(row[1])
        forward_out = advance(forward_fields[angle], forward_spectrum[angle], permittivity, cos_x, sin_x, cos_y, sin_y)
        adjoint_out = advance(adjoint_fields[angle], adjoint_spectrum[angle], permittivity, cos_x, -sin_x, cos_y, -sin_y)
        total = total + jnp.sum(forward_out[0] * adjoint_out[0] - forward_out[1] * adjoint_out[1], axis=0)
        forward_list.append(forward_out.reshape((6, NX, NY, NZ)))
        adjoint_list.append(adjoint_out.reshape((6, NX, NY, NZ)))
    tile_x = (jnp.arange(NX) // CX).astype(jnp.int32)
    tile_y = (jnp.arange(NY) // CY).astype(jnp.int32)
    tiles = tile_x[:, None] * N_GY + tile_y[None, :]
    inside = jnp.any(tiles[:, :, None] == design_tiles[None, None, :], axis=-1).astype(jnp.float32)
    gradient = total * inside[:, :, None] * (1.0 / ANGLES)
    return jnp.stack(forward_list), jnp.stack(adjoint_list), gradient
```

```python
import math

import jax
import jax.numpy as jnp
from jax import lax
from jax.experimental import pallas as pl
from jax.experimental.pallas import tpu as pltpu
from jax.sharding import PartitionSpec as P

STEPS = 3
COURANT = 0.5
OMEGA_STEP = 0.7
CX, CY, NZ = 8, 16, 128
ROWS = 24
GROUPS = 8
CHUNK = NZ // GROUPS
MESH = pl.DeviceIdType.MESH

KINDS = ((1, -1), (-1, 1), (-1, 0), (1, 0), (0, -1), (0, 1))
CORNER_A, CORNER_B, EX_MSG, PX_MSG, EY_MSG, PY_MSG = range(6)


def rotate(pair, cosine, sine):
    real_part, imag_part = pair
    return real_part * cosine - imag_part * sine, real_part * sine + imag_part * cosine


def kernel(
    ff, af, fs, as_, perm, phase, aidx, tiles,
    ft, at, grad,
    efield, hfield, coef, permbuf, phs, packed, landed,
    sx, sy, sc, rx, ry, rc,
    load_sem, send_sem, recv_sem, gsend_sem, grecv_sem,
):
    me_a = lax.axis_index("angle")
    me_x = lax.axis_index("gx")
    me_y = lax.axis_index("gy")
    n_a, n_x, n_y = GROUPS, lax.axis_size("gx"), lax.axis_size("gy")

    def shifted(kind):
        dx, dy = KINDS[kind]
        return {"gx": lax.rem(me_x + dx + n_x, n_x), "gy": lax.rem(me_y + dy + n_y, n_y)}

    def angle_peer(offset):
        return {"angle": lax.rem(me_a + offset, n_a)}

    loads = []
    count = [0]

    def load(src, dst):
        copy = pltpu.make_async_copy(src, dst, load_sem.at[count[0]])
        count[0] += 1
        copy.start()
        return copy

    field_loads = []
    for run, src in enumerate((ff, af)):
        group = []
        for x in range(CX):
            group.append(load(src.at[0, 0:6, x], efield.at[run, :, ROWS * x : ROWS * x + CY, :]))
            group.append(
                load(src.at[0, 6:12, x], hfield.at[run, :, ROWS * (x + 1) + 8 : ROWS * (x + 1) + 8 + CY, :])
            )
        field_loads.append(group)
    perm_load = load(perm, permbuf)
    spec_loads = [load(fs, ft), load(as_, at)]

    barrier = pltpu.get_barrier_semaphore()
    for kind in range(6):
        pl.semaphore_signal(barrier, inc=1, device_id=shifted(kind), device_id_type=MESH)
    for offset in range(1, n_a):
        pl.semaphore_signal(barrier, inc=1, device_id=angle_peer(offset), device_id_type=MESH)

    zero_rows = jnp.zeros((8, NZ), jnp.float32)
    for run in range(2):
        for c in range(6):
            for x in range(CX):
                efield[run, c, ROWS * x + CY : ROWS * x + CY + 8, :] = zero_rows

    lane = lax.broadcasted_iota(jnp.int32, (CY, NZ), 1)
    not_last = lane < NZ - 1
    not_first = lane > 0

    row = aidx[0]
    for axis, (place, last) in enumerate(((me_x, n_x - 1), (me_y, n_y - 1))):
        angle = jnp.full((8, NZ), phase[axis, row], jnp.float32)
        cosine, sine = jnp.cos(angle), jnp.sin(angle)
        one, zero = jnp.ones_like(cosine), jnp.zeros_like(cosine)
        ahead = (jnp.full((8, NZ), place, jnp.int32) == last)
        behind = (jnp.full((8, NZ), place, jnp.int32) == 0)
        phs[4 * axis] = jnp.where(ahead, cosine, one)
        phs[4 * axis + 1] = jnp.where(ahead, sine, zero)
        phs[4 * axis + 2] = jnp.where(behind, cosine, one)
        phs[4 * axis + 3] = jnp.where(behind, -sine, zero)

    def phase_pair(which, run, rows):
        c = phs[2 * which, 0:1, :]
        s = phs[2 * which + 1, 0:1, :]
        s = s if run == 0 else -s
        return jnp.broadcast_to(c, (rows, NZ)), jnp.broadcast_to(s, (rows, NZ))

    def e_rows(run, c, x, start=0):
        return efield[run, c, ROWS * x + start : ROWS * x + start + CY, :]

    def h_rows(run, c, x, start=0):
        base = ROWS * (x + 1) + 8 + start
        return hfield[run, c, base : base + CY, :]

    def set_h(run, c, x, value):
        base = ROWS * (x + 1) + 8
        hfield[run, c, base : base + CY, :] = value

    def next_z(value):
        return jnp.where(not_last, pltpu.roll(value, NZ - 1, 1), 0.0)

    def prev_z(value):
        return jnp.where(not_first, pltpu.roll(value, 1, 1), 0.0)

    def make(step, run, kind):
        if kind in (CORNER_A, CORNER_B):
            src, dst = sc.at[step, run, kind], rc.at[step, run, kind]
        elif kind in (EX_MSG, PX_MSG):
            src, dst = sx.at[step, run, kind - EX_MSG], rx.at[step, run, kind - EX_MSG]
        else:
            src, dst = sy.at[step, run, kind - EY_MSG], ry.at[step, run, kind - EY_MSG]
        return pltpu.make_async_remote_copy(
            src_ref=src,
            dst_ref=dst,
            send_sem=send_sem.at[step, run, kind],
            recv_sem=recv_sem.at[step, run, kind],
            device_id=shifted(kind),
            device_id_type=MESH,
        )

    def stage_e(step, run):
        for part in range(2):
            sc[step, run, CORNER_A, part : part + 1, :] = efield[run, 3 * part, ROWS * 7 : ROWS * 7 + 1, :]
            sc[step, run, CORNER_B, part : part + 1, :] = efield[run, 3 * part + 1, 15:16, :]
            for slot, c in enumerate((1, 2)):
                sx[step, run, 0, 2 * part + slot] = e_rows(run, 3 * part + c, 0)
            for slot, c in enumerate((0, 2)):
                sy[step, run, 0, 2 * part + slot] = efield[run, 3 * part + c, pl.ds(0, CX, stride=ROWS), :]

    def h_pass(step, run):
        for x in (7, 0, 1, 2, 3, 4, 5, 6):
            for part in range(2):
                b = 3 * part
                ex, ey, ez = (e_rows(run, b + c, x) for c in range(3))
                dz_dy = e_rows(run, b + 2, x, 1) - ez
                dx_dy = e_rows(run, b, x, 1) - ex
                dy_dz = next_z(ey) - ey
                dx_dz = next_z(ex) - ex
                if x < CX - 1:
                    dz_dx = e_rows(run, b + 2, x + 1) - ez
                    dy_dx = e_rows(run, b + 1, x + 1) - ey
                else:
                    dz_dx, dy_dx = -ez, -ey
                hx = h_rows(run, b, x) - COURANT * (dz_dy - dy_dz)
                hy = h_rows(run, b + 1, x) - COURANT * (dx_dz - dz_dx)
                hz = h_rows(run, b + 2, x) - COURANT * (dy_dx - dx_dy)
                set_h(run, b, x, hx)
                set_h(run, b + 1, x, hy)
                set_h(run, b + 2, x, hz)
                if x == CX - 1:
                    sx[step, run, 1, 2 * part] = hy
                    sx[step, run, 1, 2 * part + 1] = hz
        for part in range(2):
            for slot, c in enumerate((0, 2)):
                sy[step, run, 1, 2 * part + slot] = hfield[
                    run, 3 * part + c, pl.ds(ROWS + 8 + 15, CX, stride=ROWS), :
                ]

    def receive(step, run):
        for kind in range(6):
            make(step, run, kind).wait_recv()

    last_row = lax.broadcasted_iota(jnp.int32, (CY, NZ), 0) == CY - 1
    last_x = lax.broadcasted_iota(jnp.int32, (CX, NZ), 0) == CX - 1

    def halo(step, run):
        fwd_x, fwd_y = phase_pair(0, run, CY), phase_pair(2, run, CX)
        back_x, back_y = phase_pair(1, run, CY), phase_pair(3, run, CX)
        eyx = rotate((rx[step, run, 0, 0], rx[step, run, 0, 2]), *fwd_x)
        ezx = rotate((rx[step, run, 0, 1], rx[step, run, 0, 3]), *fwd_x)
        exy = rotate((ry[step, run, 0, 0], ry[step, run, 0, 2]), *fwd_y)
        ezy = rotate((ry[step, run, 0, 1], ry[step, run, 0, 3]), *fwd_y)
        rows = pl.ds(ROWS + 8 + 15, CX, stride=ROWS)
        for part in range(2):
            b = 3 * part
            set_h(run, b + 1, 7, h_rows(run, b + 1, 7) + COURANT * ezx[part])
            set_h(run, b + 2, 7, h_rows(run, b + 2, 7) - COURANT * eyx[part])
            hfield[run, b, rows, :] = hfield[run, b, rows, :] - COURANT * ezy[part]
            hfield[run, b + 2, rows, :] = hfield[run, b + 2, rows, :] + COURANT * exy[part]
        one_fwd_y = phase_pair(2, run, 1)
        one_fwd_x = phase_pair(0, run, 1)
        corner_a = rotate((rc[step, run, CORNER_A, 0:1, :], rc[step, run, CORNER_A, 1:2, :]), *one_fwd_y)
        corner_b = rotate((rc[step, run, CORNER_B, 0:1, :], rc[step, run, CORNER_B, 1:2, :]), *one_fwd_x)
        pz = tuple(
            rx[step, run, 1, 2 * part + 1]
            + jnp.where(last_row, jnp.broadcast_to(COURANT * corner_a[part], (CY, NZ)), 0.0)
            for part in range(2)
        )
        py = (rx[step, run, 1, 0], rx[step, run, 1, 2])
        hy_x, hz_x = rotate(py, *back_x), rotate(pz, *back_x)
        qz = tuple(
            ry[step, run, 1, 2 * part + 1]
            - jnp.where(last_x, jnp.broadcast_to(COURANT * corner_b[part], (CX, NZ)), 0.0)
            for part in range(2)
        )
        qx = (ry[step, run, 1, 0], ry[step, run, 1, 2])
        hx_y, hz_y = rotate(qx, *back_y), rotate(qz, *back_y)
        before = pl.ds(ROWS + 7, CX, stride=ROWS)
        first = pl.ds(0, CX, stride=ROWS)
        for part in range(2):
            b = 3 * part
            set_h(run, b + 1, -1, hy_x[part] + COURANT * e_rows(run, b + 2, 0))
            set_h(run, b + 2, -1, hz_x[part] - COURANT * e_rows(run, b + 1, 0))
            hfield[run, b, before, :] = hx_y[part] - COURANT * efield[run, b + 2, first, :]
            hfield[run, b + 2, before, :] = hz_y[part] + COURANT * efield[run, b, first, :]

    def e_pass(run):
        for x in range(CX):
            k = coef[x]
            for part in range(2):
                b = 3 * part
                hx, hy, hz = (h_rows(run, b + c, x) for c in range(3))
                cx = (hz - h_rows(run, b + 2, x, -1)) - (hy - prev_z(hy))
                cy = (hx - prev_z(hx)) - (hz - h_rows(run, b + 2, x - 1))
                cz = (hy - h_rows(run, b + 1, x - 1)) - (hx - h_rows(run, b, x, -1))
                for c, curl in enumerate((cx, cy, cz)):
                    efield[run, b + c, ROWS * x : ROWS * x + CY, :] = e_rows(run, b + c, x) + k * curl

    outs = (ft, at)

    def spectrum(step, run):
        theta = OMEGA_STEP * (step + 1)
        cw, sw = math.cos(theta), math.sin(theta)
        out = outs[run]
        for x in range(CX):
            for c in range(3):
                ec, es = e_rows(run, c, x), e_rows(run, 3 + c, x)
                out[0, c, x] = out[0, c, x] + (ec * cw - es * sw)
                out[0, 3 + c, x] = out[0, 3 + c, x] + (ec * sw + es * cw)

    for run in range(2):
        for copy in field_loads[run]:
            copy.wait()
        stage_e(0, run)
        h_pass(0, run)
    pl.semaphore_wait(barrier, 6 + n_a - 1)
    for run in range(2):
        for kind in range(6):
            make(0, run, kind).start()
    perm_load.wait()
    for x in range(CX):
        coef[x] = COURANT / permbuf[x]
    for copy in spec_loads:
        copy.wait()

    for step in range(STEPS):
        for run in range(2):
            receive(step, run)
            halo(step, run)
            e_pass(run)
            if step + 1 < STEPS:
                stage_e(step + 1, run)
                for kind in (CORNER_A, CORNER_B, EX_MSG, EY_MSG):
                    make(step + 1, run, kind).start()
                h_pass(step + 1, run)
                for kind in (PX_MSG, PY_MSG):
                    make(step + 1, run, kind).start()
        for run in range(2):
            spectrum(step, run)

    block = lane // CHUNK
    term = []
    for x in range(CX):
        total = None
        for c in range(3):
            value = ft[0, c, x] * at[0, c, x] - ft[0, 3 + c, x] * at[0, 3 + c, x]
            total = value if total is None else total + value
        term.append(total)
    for stride in (1, 2, 4):
        low = (block // stride) % 2 == 0
        fresh = list(term)
        for j in range(GROUPS):
            if (j // stride) % 2 == 0:
                a, b = term[j], term[j + stride]
                fresh[j] = jnp.where(low, a, pltpu.roll(b, CHUNK * stride, 1))
                fresh[j + stride] = jnp.where(low, pltpu.roll(a, NZ - CHUNK * stride, 1), b)
        term = fresh
    for j in range(GROUPS):
        packed[j] = term[j]

    def share(offset):
        peer = angle_peer(offset)
        return pltpu.make_async_remote_copy(
            src_ref=packed.at[peer["angle"]],
            dst_ref=landed.at[offset],
            send_sem=gsend_sem.at[offset],
            recv_sem=grecv_sem.at[offset],
            device_id=peer,
            device_id_type=MESH,
        )

    for offset in range(1, n_a):
        share(offset).start()
    own_tile = me_x * n_y + me_y
    hits = jnp.int32(0)
    for i in range(tiles.shape[0]):
        hits = hits + jnp.where(tiles[i] == own_tile, 1, 0)
    chosen = jnp.full((CY, NZ), hits, jnp.int32) > 0
    total = packed[me_a]
    for offset in range(1, n_a):
        share(offset).wait_recv()
        total = total + landed[offset]
    total = jnp.where(chosen, total * (1.0 / GROUPS), 0.0)
    for j in range(CX):
        moved = total if j == 0 else pltpu.roll(total, NZ - CHUNK * j, 1)
        grad[j] = moved[:, 0:CHUNK]

    for step in range(STEPS):
        for run in range(2):
            for kind in range(6):
                make(step, run, kind).wait_send()
    for offset in range(1, n_a):
        share(offset).wait_send()


def shards(ff, af, fs, as_, perm, phase_table, angle_index, design_tiles):
    f32 = jnp.float32
    hbm = pl.BlockSpec(memory_space=pl.ANY)
    smem = pl.BlockSpec(memory_space=pltpu.SMEM)
    vmem = pl.BlockSpec(memory_space=pltpu.VMEM)
    loads = 2 * 2 * CX + 3
    return pl.pallas_call(
        kernel,
        out_shape=(
            jax.ShapeDtypeStruct((1, 6, CX, CY, NZ), f32),
            jax.ShapeDtypeStruct((1, 6, CX, CY, NZ), f32),
            jax.ShapeDtypeStruct((CX, CY, CHUNK), f32),
        ),
        in_specs=[hbm] * 5 + [smem] * 3,
        out_specs=(vmem, vmem, vmem),
        scratch_shapes=[
            pltpu.VMEM((2, 6, CX * ROWS, NZ), f32),
            pltpu.VMEM((2, 6, (CX + 1) * ROWS, NZ), f32),
            pltpu.VMEM((CX, CY, NZ), f32),
            pltpu.VMEM((CX, CY, NZ), f32),
            pltpu.VMEM((8, 8, NZ), f32),
            pltpu.VMEM((GROUPS, CY, NZ), f32),
            pltpu.VMEM((GROUPS, CY, NZ), f32),
            pltpu.VMEM((STEPS, 2, 2, 4, CY, NZ), f32),
            pltpu.VMEM((STEPS, 2, 2, 4, CX, NZ), f32),
            pltpu.VMEM((STEPS, 2, 2, 2, NZ), f32),
            pltpu.VMEM((STEPS, 2, 2, 4, CY, NZ), f32),
            pltpu.VMEM((STEPS, 2, 2, 4, CX, NZ), f32),
            pltpu.VMEM((STEPS, 2, 2, 2, NZ), f32),
            pltpu.SemaphoreType.DMA((loads,)),
            pltpu.SemaphoreType.DMA((STEPS, 2, 6)),
            pltpu.SemaphoreType.DMA((STEPS, 2, 6)),
            pltpu.SemaphoreType.DMA((GROUPS,)),
            pltpu.SemaphoreType.DMA((GROUPS,)),
        ],
        compiler_params=pltpu.CompilerParams(collective_id=0, has_side_effects=True),
        name="fdtd",
    )(ff, af, fs, as_, perm, phase_table.T, angle_index, design_tiles)


def solution(mesh):
    in_specs = (
        P("angle", None, "gx", "gy", None),
        P("angle", None, "gx", "gy", None),
        P("angle", None, "gx", "gy", None),
        P("angle", None, "gx", "gy", None),
        P("gx", "gy", None),
        P(),
        P("angle"),
        P(),
    )
    out_specs = (
        P("angle", None, "gx", "gy", None),
        P("angle", None, "gx", "gy", None),
        P("gx", "gy", "angle"),
    )
    return jax.shard_map(shards, mesh=mesh, in_specs=in_specs, out_specs=out_specs, check_vma=False)
```

```python
import math

import jax
import jax.numpy as jnp
from jax import lax
from jax.experimental import pallas as pl
from jax.experimental.pallas import tpu as pltpu
from jax.sharding import PartitionSpec as P

STEPS = 3
COURANT = 0.5
OMEGA_STEP = 0.7
CX, CY, NZ = 8, 16, 128
ROWS = 24
GROUPS = 8
CHUNK = NZ // GROUPS
MESH = pl.DeviceIdType.MESH
LAST = STEPS - 1

KINDS = ((1, -1), (-1, 1), (-1, 0), (1, 0), (0, -1), (0, 1))
CORNER_A, CORNER_B, EX_MSG, PX_MSG, EY_MSG, PY_MSG = range(6)
DIRECT = (EX_MSG, PX_MSG, EY_MSG, PY_MSG)
CORNERS = (CORNER_A, CORNER_B)

E_FIRST = pl.ds(0, CX, stride=ROWS)
E_LAST = pl.ds(CY - 1, CX, stride=ROWS)
E_LAST_NEXT_X = pl.ds(ROWS + CY - 1, CX, stride=ROWS)
H_LAST = pl.ds(ROWS + 8 + CY - 1, CX, stride=ROWS)
FIRST = pl.ds(0, CX, stride=CY)
FINAL = pl.ds(CY - 1, CX, stride=CY)


def rotate(pair, cosine, sine):
    real_part, imag_part = pair
    return real_part * cosine - imag_part * sine, real_part * sine + imag_part * cosine


def kernel(
    ff, af, fs, as_, perm, phase, aidx, tiles,
    ft, at, grad,
    efield, hfield, coef, phs, terms, packed, landed,
    sx, sy, sc, rx, ry, rc,
    load_sem, send_sem, recv_sem, gsend_sem, grecv_sem, ready_sem,
):
    me_a = lax.axis_index("angle")
    me_x = lax.axis_index("gx")
    me_y = lax.axis_index("gy")
    n_a, n_x, n_y = GROUPS, lax.axis_size("gx"), lax.axis_size("gy")

    def shifted(kind):
        dx, dy = KINDS[kind]
        return {"gx": lax.rem(me_x + dx + n_x, n_x), "gy": lax.rem(me_y + dy + n_y, n_y)}

    def angle_peer(offset):
        return {"angle": lax.rem(me_a + offset, n_a)}

    barrier = pltpu.get_barrier_semaphore()
    for kind in DIRECT:
        pl.semaphore_signal(barrier, inc=1, device_id=shifted(kind), device_id_type=MESH)
    for offset in range(1, n_a):
        pl.semaphore_signal(barrier, inc=1, device_id=angle_peer(offset), device_id_type=MESH)

    count = [0]

    def load(src, dst):
        copy = pltpu.make_async_copy(src, dst, load_sem.at[count[0]])
        count[0] += 1
        copy.start()
        return copy

    field_loads = []
    for run, src in enumerate((ff, af)):
        group = []
        for x in range(CX):
            group.append(load(src.at[0, 0:6, x], efield.at[run, :, ROWS * x : ROWS * x + CY, :]))
            base = ROWS * (x + 1) + 8
            group.append(load(src.at[0, 6:12, x], hfield.at[run, :, base : base + CY, :]))
        field_loads.append(group)
    perm_load = load(perm, coef)
    spec_loads = [load(fs, ft), load(as_, at)]

    zero_rows = jnp.zeros((8, NZ), jnp.float32)
    zero_plane = jnp.zeros((CY, NZ), jnp.float32)
    for run in range(2):
        for c in range(6):
            for x in range(CX):
                efield[run, c, ROWS * x + CY : ROWS * (x + 1), :] = zero_rows
                hfield[run, c, ROWS * (x + 1) : ROWS * (x + 1) + 8, :] = zero_rows
            efield[run, c, ROWS * CX : ROWS * CX + CY, :] = zero_plane
            hfield[run, c, 8 : 8 + CY, :] = zero_plane

    lane = lax.broadcasted_iota(jnp.int32, (CY, NZ), 1)
    not_last = lane < NZ - 1
    not_first = lane > 0
    row_index = lax.broadcasted_iota(jnp.int32, (CY, NZ), 0)
    x_index = lax.broadcasted_iota(jnp.int32, (CX, NZ), 0)

    row = aidx[0]
    for axis, (place, last) in enumerate(((me_x, n_x - 1), (me_y, n_y - 1))):
        angle = jnp.full((8, NZ), phase[axis, row], jnp.float32)
        cosine, sine = jnp.cos(angle), jnp.sin(angle)
        one, zero = jnp.ones_like(cosine), jnp.zeros_like(cosine)
        ahead = jnp.full((8, NZ), place, jnp.int32) == last
        behind = jnp.full((8, NZ), place, jnp.int32) == 0
        phs[4 * axis] = jnp.where(ahead, cosine, one)
        phs[4 * axis + 1] = jnp.where(ahead, sine, zero)
        phs[4 * axis + 2] = jnp.where(behind, cosine, one)
        phs[4 * axis + 3] = jnp.where(behind, -sine, zero)

    def phase_pair(which, run, rows):
        c = phs[2 * which, 0:1, :]
        s = phs[2 * which + 1, 0:1, :]
        s = s if run == 0 else -s
        return jnp.broadcast_to(c, (rows, NZ)), jnp.broadcast_to(s, (rows, NZ))

    def e_rows(run, c, x, start=0):
        return efield[run, c, ROWS * x + start : ROWS * x + start + CY, :]

    def set_e(run, c, x, value):
        efield[run, c, ROWS * x : ROWS * x + CY, :] = value

    def h_rows(run, c, x, start=0):
        base = ROWS * (x + 1) + 8 + start
        return hfield[run, c, base : base + CY, :]

    def set_h(run, c, x, value):
        base = ROWS * (x + 1) + 8
        hfield[run, c, base : base + CY, :] = value

    def next_z(value):
        return jnp.where(not_last[: value.shape[0]], pltpu.roll(value, NZ - 1, 1), 0.0)

    def prev_z(value):
        return jnp.where(not_first[: value.shape[0]], pltpu.roll(value, 1, 1), 0.0)

    def make(step, run, kind):
        if kind in CORNERS:
            src, dst = sc.at[step, run, kind], rc.at[step, run, kind]
        elif kind in (EX_MSG, PX_MSG):
            src, dst = sx.at[step, run, kind - EX_MSG], rx.at[step, run, kind - EX_MSG]
        else:
            src, dst = sy.at[step, run, kind - EY_MSG], ry.at[step, run, kind - EY_MSG]
        return pltpu.make_async_remote_copy(
            src_ref=src,
            dst_ref=dst,
            send_sem=send_sem.at[step, run, kind],
            recv_sem=recv_sem.at[step, run, kind],
            device_id=shifted(kind),
            device_id_type=MESH,
        )

    def stage_e(step, run):
        for part in range(2):
            b = 3 * part
            sc[step, run, CORNER_A, part : part + 1, :] = efield[run, b, ROWS * 7 : ROWS * 7 + 1, :]
            sc[step, run, CORNER_B, part : part + 1, :] = efield[run, b + 1, CY - 1 : CY, :]
            for slot, c in enumerate((1, 2)):
                sx[step, run, 0, 2 * part + slot] = e_rows(run, b + c, 0)
            for slot, c in enumerate((0, 2)):
                sy[step, run, 0, 2 * part + slot] = efield[run, b + c, E_FIRST, :]

    def h_value(run, part, x):
        b = 3 * part
        ex, ey, ez = (e_rows(run, b + c, x) for c in range(3))
        dz_dy = e_rows(run, b + 2, x, 1) - ez
        dx_dy = e_rows(run, b, x, 1) - ex
        dy_dz = next_z(ey) - ey
        dx_dz = next_z(ex) - ex
        dz_dx = e_rows(run, b + 2, x + 1) - ez
        dy_dx = e_rows(run, b + 1, x + 1) - ey
        hx = h_rows(run, b, x) - COURANT * (dz_dy - dy_dz)
        hy = h_rows(run, b + 1, x) - COURANT * (dx_dz - dz_dx)
        hz = h_rows(run, b + 2, x) - COURANT * (dy_dx - dx_dy)
        return hx, hy, hz

    def stage_h(step, run):
        for part in range(2):
            b = 3 * part
            ex, ey, ez = (efield[run, b + c, E_LAST, :] for c in range(3))
            ey_next = efield[run, b + 1, E_LAST_NEXT_X, :]
            hx = hfield[run, b, H_LAST, :] + COURANT * (ez + (next_z(ey) - ey))
            hz = hfield[run, b + 2, H_LAST, :] - COURANT * ((ey_next - ey) + ex)
            sy[step, run, 1, 2 * part] = hx
            sy[step, run, 1, 2 * part + 1] = hz
        for part in range(2):
            b = 3 * part
            hx, hy, hz = h_value(run, part, CX - 1)
            sx[step, run, 1, 2 * part] = hy
            sx[step, run, 1, 2 * part + 1] = hz
            for c, value in enumerate((hx, hy, hz)):
                set_h(run, b + c, CX - 1, value)

    outs = (ft, at)

    def turn(step):
        theta = OMEGA_STEP * (step + 1)
        return math.cos(theta), math.sin(theta)

    def bulk(step, run):
        for x in range(CX - 1):
            for part in range(2):
                for c, value in enumerate(h_value(run, part, x)):
                    set_h(run, 3 * part + c, x, value)
        out = outs[run]
        for x in range(CX):
            k = coef[x]
            old, new = [], []
            for part in range(2):
                b = 3 * part
                hx, hy, hz = (h_rows(run, b + c, x) for c in range(3))
                curl_x = (hz - h_rows(run, b + 2, x, -1)) - (hy - prev_z(hy))
                curl_y = (hx - prev_z(hx)) - (hz - h_rows(run, b + 2, x - 1))
                curl_z = (hy - h_rows(run, b + 1, x - 1)) - (hx - h_rows(run, b, x, -1))
                for c, curl in enumerate((curl_x, curl_y, curl_z)):
                    e = e_rows(run, b + c, x)
                    old.append(e)
                    new.append(e + k * curl)
            rows = slice(CY * x, CY * (x + 1))
            for c in range(3):
                real, imag = None, None
                if step > 0:
                    real, imag = rotate((old[c], old[3 + c]), *turn(step - 1))
                if step == LAST:
                    more = rotate((new[c], new[3 + c]), *turn(step))
                    real = more[0] if real is None else real + more[0]
                    imag = more[1] if imag is None else imag + more[1]
                if real is not None:
                    out[0, c, rows, :] = out[0, c, rows, :] + real
                    out[0, 3 + c, rows, :] = out[0, 3 + c, rows, :] + imag
            if step < LAST:
                for c in range(6):
                    set_e(run, c, x, new[c])

    def receive(step, run):
        for kind in range(6):
            make(step, run, kind).wait_recv()

    def arrive(step, run):
        fwd_x, fwd_y = phase_pair(0, run, CY), phase_pair(2, run, CX)
        back_x, back_y = phase_pair(1, run, CY), phase_pair(3, run, CX)
        one_x, one_y = phase_pair(0, run, 1), phase_pair(2, run, 1)
        eyx = rotate((rx[step, run, 0, 0], rx[step, run, 0, 2]), *fwd_x)
        ezx = rotate((rx[step, run, 0, 1], rx[step, run, 0, 3]), *fwd_x)
        exy = rotate((ry[step, run, 0, 0], ry[step, run, 0, 2]), *fwd_y)
        ezy = rotate((ry[step, run, 0, 1], ry[step, run, 0, 3]), *fwd_y)
        corner_a = rotate((rc[step, run, CORNER_A, 0:1, :], rc[step, run, CORNER_A, 1:2, :]), *one_y)
        corner_b = rotate((rc[step, run, CORNER_B, 0:1, :], rc[step, run, CORNER_B, 1:2, :]), *one_x)
        pz = tuple(
            rx[step, run, 1, 2 * part + 1]
            + jnp.where(row_index == CY - 1, jnp.broadcast_to(COURANT * corner_a[part], (CY, NZ)), 0.0)
            for part in range(2)
        )
        qz = tuple(
            ry[step, run, 1, 2 * part + 1]
            - jnp.where(x_index == CX - 1, jnp.broadcast_to(COURANT * corner_b[part], (CX, NZ)), 0.0)
            for part in range(2)
        )
        hy_x = rotate((rx[step, run, 1, 0], rx[step, run, 1, 2]), *back_x)
        hz_x = rotate(pz, *back_x)
        hx_y = rotate((ry[step, run, 1, 0], ry[step, run, 1, 2]), *back_y)
        hz_y = rotate(qz, *back_y)
        k_first, k_last = coef[0], coef[CX - 1]
        k_row_first, k_row_last = coef.reshape(CX * CY, NZ)[FIRST, :], coef.reshape(CX * CY, NZ)[FINAL, :]
        plane_last, row_last, plane_first, row_first = [], [], [], []
        for part in range(2):
            b = 3 * part
            dy_plane, dz_plane = COURANT * ezx[part], -COURANT * eyx[part]
            dx_row, dz_row = -COURANT * ezy[part], COURANT * exy[part]
            if step < LAST:
                set_h(run, b + 1, CX - 1, h_rows(run, b + 1, CX - 1) + dy_plane)
                set_h(run, b + 2, CX - 1, h_rows(run, b + 2, CX - 1) + dz_plane)
                hfield[run, b, H_LAST, :] = hfield[run, b, H_LAST, :] + dx_row
                hfield[run, b + 2, H_LAST, :] = hfield[run, b + 2, H_LAST, :] + dz_row
            dz_above = jnp.where(row_index > 0, pltpu.roll(dz_plane, 1, 0), 0.0)
            dz_before = jnp.where(x_index > 0, pltpu.roll(dz_row, 1, 0), 0.0)
            plane_last += [
                k_last * ((dz_plane - dz_above) - (dy_plane - prev_z(dy_plane))),
                -(k_last * dz_plane),
                k_last * dy_plane,
            ]
            row_last += [
                k_row_last * dz_row,
                k_row_last * ((dx_row - prev_z(dx_row)) - (dz_row - dz_before)),
                -(k_row_last * dx_row),
            ]
            hy = hy_x[part] + COURANT * sx[step, run, 0, 2 * part + 1]
            hz = hz_x[part] - COURANT * sx[step, run, 0, 2 * part]
            plane_first += [None, k_first * hz, -(k_first * hy)]
            hx = hx_y[part] - COURANT * sy[step, run, 0, 2 * part + 1]
            hz = hz_y[part] + COURANT * sy[step, run, 0, 2 * part]
            row_first += [-(k_row_first * hz), None, k_row_first * hx]
        if step < LAST:
            for c in range(6):
                set_e(run, c, CX - 1, e_rows(run, c, CX - 1) + plane_last[c])
            for c in range(6):
                if plane_first[c] is not None:
                    set_e(run, c, 0, e_rows(run, c, 0) + plane_first[c])
            for c in range(6):
                efield[run, c, E_LAST, :] = efield[run, c, E_LAST, :] + row_last[c]
            for c in range(6):
                if row_first[c] is not None:
                    efield[run, c, E_FIRST, :] = efield[run, c, E_FIRST, :] + row_first[c]
        else:
            out = outs[run]
            for rows, gains in (
                (slice(CY * (CX - 1), CY * CX), plane_last),
                (slice(0, CY), plane_first),
                (FINAL, row_last),
                (FIRST, row_first),
            ):
                for c in range(3):
                    if gains[c] is not None:
                        real, imag = rotate((gains[c], gains[3 + c]), *turn(step))
                        out[0, c, rows, :] = out[0, c, rows, :] + real
                        out[0, 3 + c, rows, :] = out[0, 3 + c, rows, :] + imag

    def term(rows):
        total = None
        for c in range(3):
            value = ft[0, c, rows, :] * at[0, c, rows, :] - ft[0, 3 + c, rows, :] * at[0, 3 + c, rows, :]
            total = value if total is None else total + value
        return total

    for run in range(2):
        for copy in field_loads[run]:
            copy.wait()
        stage_e(0, run)
        stage_h(0, run)
    pl.semaphore_wait(barrier, len(DIRECT) + n_a - 1)
    for run in range(2):
        for kind in DIRECT:
            make(0, run, kind).start()
    for kind in (EY_MSG, PY_MSG):
        pl.semaphore_signal(ready_sem, inc=1, device_id=shifted(kind), device_id_type=MESH)
    perm_load.wait()
    for x in range(CX):
        coef[x] = COURANT / coef[x]
    bulk(0, 0)
    pl.semaphore_wait(ready_sem, 2)
    for run in range(2):
        for kind in CORNERS:
            make(0, run, kind).start()
    bulk(0, 1)
    for copy in spec_loads:
        copy.wait()

    for step in range(STEPS):
        for run in range(2):
            receive(step, run)
            arrive(step, run)
            if step < LAST:
                stage_e(step + 1, run)
                for kind in (CORNER_A, CORNER_B, EX_MSG, EY_MSG):
                    make(step + 1, run, kind).start()
                stage_h(step + 1, run)
                for kind in (PX_MSG, PY_MSG):
                    make(step + 1, run, kind).start()
                bulk(step + 1, run)
        if step == LAST - 1:
            for x in range(1, CX - 1):
                terms[x] = term(slice(CY * x, CY * (x + 1)))

    flat = terms.reshape(CX * CY, NZ)
    flat[FIRST, :] = term(FIRST)
    flat[FINAL, :] = term(FINAL)
    block = lane // CHUNK
    planes = [term(slice(CY * x, CY * (x + 1))) if x in (0, CX - 1) else terms[x] for x in range(CX)]
    for stride in (1, 2, 4):
        low = (block // stride) % 2 == 0
        fresh = list(planes)
        for j in range(GROUPS):
            if (j // stride) % 2 == 0:
                a, b = planes[j], planes[j + stride]
                fresh[j] = jnp.where(low, a, pltpu.roll(b, CHUNK * stride, 1))
                fresh[j + stride] = jnp.where(low, pltpu.roll(a, NZ - CHUNK * stride, 1), b)
        planes = fresh
    for j in range(GROUPS):
        packed[j] = planes[j]

    def share(offset):
        peer = angle_peer(offset)
        return pltpu.make_async_remote_copy(
            src_ref=packed.at[peer["angle"]],
            dst_ref=landed.at[offset],
            send_sem=gsend_sem.at[offset],
            recv_sem=grecv_sem.at[offset],
            device_id=peer,
            device_id_type=MESH,
        )

    for offset in range(1, n_a):
        share(offset).start()
    for step in range(STEPS):
        for run in range(2):
            for kind in range(6):
                make(step, run, kind).wait_send()
    own_tile = me_x * n_y + me_y
    hits = jnp.int32(0)
    for i in range(tiles.shape[0]):
        hits = hits + jnp.where(tiles[i] == own_tile, 1, 0)
    chosen = jnp.full((CY, NZ), hits, jnp.int32) > 0
    total = packed[me_a]
    for offset in range(1, n_a):
        share(offset).wait_recv()
        total = total + landed[offset]
    total = jnp.where(chosen, total * (1.0 / GROUPS), 0.0)
    for j in range(CX):
        moved = total if j == 0 else pltpu.roll(total, NZ - CHUNK * j, 1)
        grad[j] = moved[:, 0:CHUNK]
    for offset in range(1, n_a):
        share(offset).wait_send()


def write_out(ft, at, grad, ft_out, at_out, grad_out, sem):
    copies = [
        pltpu.make_async_copy(src, dst, sem.at[i])
        for i, (src, dst) in enumerate(((ft, ft_out), (at, at_out), (grad, grad_out)))
    ]
    for copy in copies:
        copy.start()
    for copy in copies:
        copy.wait()


def shards(ff, af, fs, as_, perm, phase_table, angle_index, design_tiles):
    f32 = jnp.float32
    hbm = pl.BlockSpec(memory_space=pl.ANY)
    smem = pl.BlockSpec(memory_space=pltpu.SMEM)
    vmem = pl.BlockSpec(memory_space=pltpu.VMEM)
    loads = 2 * 2 * CX + 3
    flat = (1, 6, CX * CY, NZ)
    cells = (1, 6, CX, CY, NZ)
    held = pl.pallas_call(
        kernel,
        out_shape=(pltpu.VMEM(flat, f32), pltpu.VMEM(flat, f32), pltpu.VMEM((CX, CY, CHUNK), f32)),
        in_specs=[hbm] * 5 + [smem] * 3,
        out_specs=(vmem, vmem, vmem),
        scratch_shapes=[
            pltpu.VMEM((2, 6, (CX + 1) * ROWS, NZ), f32),
            pltpu.VMEM((2, 6, (CX + 1) * ROWS, NZ), f32),
            pltpu.VMEM((CX, CY, NZ), f32),
            pltpu.VMEM((8, 8, NZ), f32),
            pltpu.VMEM((CX, CY, NZ), f32),
            pltpu.VMEM((GROUPS, CY, NZ), f32),
            pltpu.VMEM((GROUPS, CY, NZ), f32),
            pltpu.VMEM((STEPS, 2, 2, 4, CY, NZ), f32),
            pltpu.VMEM((STEPS, 2, 2, 4, CX, NZ), f32),
            pltpu.VMEM((STEPS, 2, 2, 2, NZ), f32),
            pltpu.VMEM((STEPS, 2, 2, 4, CY, NZ), f32),
            pltpu.VMEM((STEPS, 2, 2, 4, CX, NZ), f32),
            pltpu.VMEM((STEPS, 2, 2, 2, NZ), f32),
            pltpu.SemaphoreType.DMA((loads,)),
            pltpu.SemaphoreType.DMA((STEPS, 2, 6)),
            pltpu.SemaphoreType.DMA((STEPS, 2, 6)),
            pltpu.SemaphoreType.DMA((GROUPS,)),
            pltpu.SemaphoreType.DMA((GROUPS,)),
            pltpu.SemaphoreType.REGULAR,
        ],
        compiler_params=pltpu.CompilerParams(collective_id=0, has_side_effects=True),
        name="fdtd",
    )(ff, af, fs.reshape(flat), as_.reshape(flat), perm, phase_table.T, angle_index, design_tiles)
    ft, at, grad = pl.pallas_call(
        write_out,
        out_shape=(
            jax.ShapeDtypeStruct(flat, f32),
            jax.ShapeDtypeStruct(flat, f32),
            jax.ShapeDtypeStruct((CX, CY, CHUNK), f32),
        ),
        in_specs=[hbm] * 3,
        out_specs=(hbm,) * 3,
        scratch_shapes=[pltpu.SemaphoreType.DMA((3,))],
        name="write_out",
    )(*(pltpu.with_memory_space_constraint(a, pltpu.VMEM) for a in held))
    return ft.reshape(cells), at.reshape(cells), grad


def solution(mesh):
    in_specs = (
        P("angle", None, "gx", "gy", None),
        P("angle", None, "gx", "gy", None),
        P("angle", None, "gx", "gy", None),
        P("angle", None, "gx", "gy", None),
        P("gx", "gy", None),
        P(),
        P("angle"),
        P(),
    )
    out_specs = (
        P("angle", None, "gx", "gy", None),
        P("angle", None, "gx", "gy", None),
        P("gx", "gy", "angle"),
    )
    return jax.shard_map(shards, mesh=mesh, in_specs=in_specs, out_specs=out_specs, check_vma=False)
```

```python
import math

import jax
import jax.numpy as jnp
from jax import lax
from jax.experimental import pallas as pl
from jax.experimental.pallas import tpu as pltpu
from jax.sharding import PartitionSpec as P

STEPS = 3
COURANT = 0.5
OMEGA_STEP = 0.7
CX, CY, NZ = 8, 16, 128
ROWS = 24
GROUPS = 8
CHUNK = NZ // GROUPS
MESH = pl.DeviceIdType.MESH
LAST = STEPS - 1

KINDS = ((1, -1), (-1, 1), (-1, 0), (1, 0), (0, -1), (0, 1))
CORNER_A, CORNER_B, EX_MSG, PX_MSG, EY_MSG, PY_MSG = range(6)
DIRECT = (EY_MSG, PY_MSG, EX_MSG, PX_MSG)
CORNERS = (CORNER_A, CORNER_B)

E_FIRST = pl.ds(0, CX, stride=ROWS)
E_LAST = pl.ds(CY - 1, CX, stride=ROWS)
E_LAST_NEXT_X = pl.ds(ROWS + CY - 1, CX, stride=ROWS)
H_LAST = pl.ds(ROWS + 8 + CY - 1, CX, stride=ROWS)
FIRST = pl.ds(0, CX, stride=CY)
FINAL = pl.ds(CY - 1, CX, stride=CY)


def rotate(pair, cosine, sine):
    real_part, imag_part = pair
    return real_part * cosine - imag_part * sine, real_part * sine + imag_part * cosine


def kernel(
    ff, af, fs, as_, perm, phase_in, aidx_in, tiles_in,
    ft, at, grad,
    efield, hfield, coef, phs, terms, packed, landed,
    sx, sy, sc, rx, ry, rc,
    phase, aidx, tiles,
    load_sem, send_sem, recv_sem, gsend_sem, grecv_sem, ready_sem,
):
    me_a = lax.axis_index("angle")
    me_x = lax.axis_index("gx")
    me_y = lax.axis_index("gy")
    n_a, n_x, n_y = GROUPS, lax.axis_size("gx"), lax.axis_size("gy")

    def shifted(kind):
        dx, dy = KINDS[kind]
        return {"gx": lax.rem(me_x + dx + n_x, n_x), "gy": lax.rem(me_y + dy + n_y, n_y)}

    def angle_peer(offset):
        return {"angle": lax.rem(me_a + offset, n_a)}

    barrier = pltpu.get_barrier_semaphore()
    for kind in DIRECT:
        pl.semaphore_signal(barrier, inc=1, device_id=shifted(kind), device_id_type=MESH)
    for offset in range(1, n_a):
        pl.semaphore_signal(barrier, inc=1, device_id=angle_peer(offset), device_id_type=MESH)

    count = [0]

    def load(src, dst):
        copy = pltpu.make_async_copy(src, dst, load_sem.at[count[0]])
        count[0] += 1
        copy.start()
        return copy

    small_loads = [load(aidx_in, aidx), load(phase_in, phase), load(tiles_in, tiles)]
    field_loads = []
    for run, src in enumerate((ff, af)):
        group = []
        for x in range(CX):
            group.append(load(src.at[0, 0:6, x], efield.at[run, :, ROWS * x : ROWS * x + CY, :]))
            base = ROWS * (x + 1) + 8
            group.append(load(src.at[0, 6:12, x], hfield.at[run, :, base : base + CY, :]))
        field_loads.append(group)
    perm_load = load(perm, coef)
    spec_loads = [load(fs, ft), load(as_, at)]

    zero_rows = jnp.zeros((8, NZ), jnp.float32)
    zero_plane = jnp.zeros((CY, NZ), jnp.float32)
    for run in range(2):
        for c in range(6):
            for x in range(CX):
                efield[run, c, ROWS * x + CY : ROWS * (x + 1), :] = zero_rows
                hfield[run, c, ROWS * (x + 1) : ROWS * (x + 1) + 8, :] = zero_rows
            efield[run, c, ROWS * CX : ROWS * CX + CY, :] = zero_plane
            hfield[run, c, 8 : 8 + CY, :] = zero_plane

    lane = lax.broadcasted_iota(jnp.int32, (CY, NZ), 1)
    not_last = lane < NZ - 1
    not_first = lane > 0
    row_index = lax.broadcasted_iota(jnp.int32, (CY, NZ), 0)
    x_index = lax.broadcasted_iota(jnp.int32, (CX, NZ), 0)

    for copy in small_loads:
        copy.wait()
    row = aidx[0]
    for axis, (place, last) in enumerate(((me_x, n_x - 1), (me_y, n_y - 1))):
        angle = jnp.full((8, NZ), phase[axis, row], jnp.float32)
        cosine, sine = jnp.cos(angle), jnp.sin(angle)
        one, zero = jnp.ones_like(cosine), jnp.zeros_like(cosine)
        ahead = jnp.full((8, NZ), place, jnp.int32) == last
        behind = jnp.full((8, NZ), place, jnp.int32) == 0
        phs[4 * axis] = jnp.where(ahead, cosine, one)
        phs[4 * axis + 1] = jnp.where(ahead, sine, zero)
        phs[4 * axis + 2] = jnp.where(behind, cosine, one)
        phs[4 * axis + 3] = jnp.where(behind, -sine, zero)

    def phase_pair(which, run, rows):
        c = phs[2 * which, 0:1, :]
        s = phs[2 * which + 1, 0:1, :]
        s = s if run == 0 else -s
        return jnp.broadcast_to(c, (rows, NZ)), jnp.broadcast_to(s, (rows, NZ))

    def e_rows(run, c, x, start=0):
        return efield[run, c, ROWS * x + start : ROWS * x + start + CY, :]

    def set_e(run, c, x, value):
        efield[run, c, ROWS * x : ROWS * x + CY, :] = value

    def h_rows(run, c, x, start=0):
        base = ROWS * (x + 1) + 8 + start
        return hfield[run, c, base : base + CY, :]

    def set_h(run, c, x, value):
        base = ROWS * (x + 1) + 8
        hfield[run, c, base : base + CY, :] = value

    def next_z(value):
        return jnp.where(not_last[: value.shape[0]], pltpu.roll(value, NZ - 1, 1), 0.0)

    def prev_z(value):
        return jnp.where(not_first[: value.shape[0]], pltpu.roll(value, 1, 1), 0.0)

    def make(step, run, kind):
        if kind in CORNERS:
            src, dst = sc.at[step, run, kind], rc.at[step, run, kind]
        elif kind in (EX_MSG, PX_MSG):
            src, dst = sx.at[step, run, kind - EX_MSG], rx.at[step, run, kind - EX_MSG]
        else:
            src, dst = sy.at[step, run, kind - EY_MSG], ry.at[step, run, kind - EY_MSG]
        return pltpu.make_async_remote_copy(
            src_ref=src,
            dst_ref=dst,
            send_sem=send_sem.at[step, run, kind],
            recv_sem=recv_sem.at[step, run, kind],
            device_id=shifted(kind),
            device_id_type=MESH,
        )

    def stage_e(step, run):
        for part in range(2):
            b = 3 * part
            sc[step, run, CORNER_A, part : part + 1, :] = efield[run, b, ROWS * 7 : ROWS * 7 + 1, :]
            sc[step, run, CORNER_B, part : part + 1, :] = efield[run, b + 1, CY - 1 : CY, :]
            for slot, c in enumerate((1, 2)):
                sx[step, run, 0, 2 * part + slot] = e_rows(run, b + c, 0)
            for slot, c in enumerate((0, 2)):
                sy[step, run, 0, 2 * part + slot] = efield[run, b + c, E_FIRST, :]

    def h_value(run, part, x):
        b = 3 * part
        ex, ey, ez = (e_rows(run, b + c, x) for c in range(3))
        dz_dy = e_rows(run, b + 2, x, 1) - ez
        dx_dy = e_rows(run, b, x, 1) - ex
        dy_dz = next_z(ey) - ey
        dx_dz = next_z(ex) - ex
        dz_dx = e_rows(run, b + 2, x + 1) - ez
        dy_dx = e_rows(run, b + 1, x + 1) - ey
        hx = h_rows(run, b, x) - COURANT * (dz_dy - dy_dz)
        hy = h_rows(run, b + 1, x) - COURANT * (dx_dz - dz_dx)
        hz = h_rows(run, b + 2, x) - COURANT * (dy_dx - dx_dy)
        return hx, hy, hz

    def stage_h(step, run):
        for part in range(2):
            b = 3 * part
            ex, ey, ez = (efield[run, b + c, E_LAST, :] for c in range(3))
            ey_next = efield[run, b + 1, E_LAST_NEXT_X, :]
            hx = hfield[run, b, H_LAST, :] + COURANT * (ez + (next_z(ey) - ey))
            hz = hfield[run, b + 2, H_LAST, :] - COURANT * ((ey_next - ey) + ex)
            sy[step, run, 1, 2 * part] = hx
            sy[step, run, 1, 2 * part + 1] = hz
        for part in range(2):
            b = 3 * part
            hx, hy, hz = h_value(run, part, CX - 1)
            sx[step, run, 1, 2 * part] = hy
            sx[step, run, 1, 2 * part + 1] = hz
            for c, value in enumerate((hx, hy, hz)):
                set_h(run, b + c, CX - 1, value)

    outs = (ft, at)

    def turn(step):
        theta = OMEGA_STEP * (step + 1)
        return math.cos(theta), math.sin(theta)

    def bulk(step, run):
        for x in range(CX - 1):
            for part in range(2):
                for c, value in enumerate(h_value(run, part, x)):
                    set_h(run, 3 * part + c, x, value)
        out = outs[run]
        for x in range(CX):
            k = coef[x]
            old, new = [], []
            for part in range(2):
                b = 3 * part
                hx, hy, hz = (h_rows(run, b + c, x) for c in range(3))
                curl_x = (hz - h_rows(run, b + 2, x, -1)) - (hy - prev_z(hy))
                curl_y = (hx - prev_z(hx)) - (hz - h_rows(run, b + 2, x - 1))
                curl_z = (hy - h_rows(run, b + 1, x - 1)) - (hx - h_rows(run, b, x, -1))
                for c, curl in enumerate((curl_x, curl_y, curl_z)):
                    e = e_rows(run, b + c, x)
                    old.append(e)
                    new.append(e + k * curl)
            rows = slice(CY * x, CY * (x + 1))
            for c in range(3):
                real, imag = None, None
                if step > 0:
                    real, imag = rotate((old[c], old[3 + c]), *turn(step - 1))
                if step == LAST:
                    more = rotate((new[c], new[3 + c]), *turn(step))
                    real = more[0] if real is None else real + more[0]
                    imag = more[1] if imag is None else imag + more[1]
                if real is not None:
                    out[0, c, rows, :] = out[0, c, rows, :] + real
                    out[0, 3 + c, rows, :] = out[0, 3 + c, rows, :] + imag
            if step < LAST:
                for c in range(6):
                    set_e(run, c, x, new[c])

    def receive(step, run):
        for kind in range(6):
            make(step, run, kind).wait_recv()

    def arrive(step, run):
        fwd_x, fwd_y = phase_pair(0, run, CY), phase_pair(2, run, CX)
        back_x, back_y = phase_pair(1, run, CY), phase_pair(3, run, CX)
        one_x, one_y = phase_pair(0, run, 1), phase_pair(2, run, 1)
        eyx = rotate((rx[step, run, 0, 0], rx[step, run, 0, 2]), *fwd_x)
        ezx = rotate((rx[step, run, 0, 1], rx[step, run, 0, 3]), *fwd_x)
        exy = rotate((ry[step, run, 0, 0], ry[step, run, 0, 2]), *fwd_y)
        ezy = rotate((ry[step, run, 0, 1], ry[step, run, 0, 3]), *fwd_y)
        corner_a = rotate((rc[step, run, CORNER_A, 0:1, :], rc[step, run, CORNER_A, 1:2, :]), *one_y)
        corner_b = rotate((rc[step, run, CORNER_B, 0:1, :], rc[step, run, CORNER_B, 1:2, :]), *one_x)
        pz = tuple(
            rx[step, run, 1, 2 * part + 1]
            + jnp.where(row_index == CY - 1, jnp.broadcast_to(COURANT * corner_a[part], (CY, NZ)), 0.0)
            for part in range(2)
        )
        qz = tuple(
            ry[step, run, 1, 2 * part + 1]
            - jnp.where(x_index == CX - 1, jnp.broadcast_to(COURANT * corner_b[part], (CX, NZ)), 0.0)
            for part in range(2)
        )
        hy_x = rotate((rx[step, run, 1, 0], rx[step, run, 1, 2]), *back_x)
        hz_x = rotate(pz, *back_x)
        hx_y = rotate((ry[step, run, 1, 0], ry[step, run, 1, 2]), *back_y)
        hz_y = rotate(qz, *back_y)
        k_first, k_last = coef[0], coef[CX - 1]
        k_row_first, k_row_last = coef.reshape(CX * CY, NZ)[FIRST, :], coef.reshape(CX * CY, NZ)[FINAL, :]
        plane_last, row_last, plane_first, row_first = [], [], [], []
        for part in range(2):
            b = 3 * part
            dy_plane, dz_plane = COURANT * ezx[part], -COURANT * eyx[part]
            dx_row, dz_row = -COURANT * ezy[part], COURANT * exy[part]
            if step < LAST:
                set_h(run, b + 1, CX - 1, h_rows(run, b + 1, CX - 1) + dy_plane)
                set_h(run, b + 2, CX - 1, h_rows(run, b + 2, CX - 1) + dz_plane)
                hfield[run, b, H_LAST, :] = hfield[run, b, H_LAST, :] + dx_row
                hfield[run, b + 2, H_LAST, :] = hfield[run, b + 2, H_LAST, :] + dz_row
            dz_above = jnp.where(row_index > 0, pltpu.roll(dz_plane, 1, 0), 0.0)
            dz_before = jnp.where(x_index > 0, pltpu.roll(dz_row, 1, 0), 0.0)
            plane_last += [
                k_last * ((dz_plane - dz_above) - (dy_plane - prev_z(dy_plane))),
                -(k_last * dz_plane),
                k_last * dy_plane,
            ]
            row_last += [
                k_row_last * dz_row,
                k_row_last * ((dx_row - prev_z(dx_row)) - (dz_row - dz_before)),
                -(k_row_last * dx_row),
            ]
            hy = hy_x[part] + COURANT * sx[step, run, 0, 2 * part + 1]
            hz = hz_x[part] - COURANT * sx[step, run, 0, 2 * part]
            plane_first += [None, k_first * hz, -(k_first * hy)]
            hx = hx_y[part] - COURANT * sy[step, run, 0, 2 * part + 1]
            hz = hz_y[part] + COURANT * sy[step, run, 0, 2 * part]
            row_first += [-(k_row_first * hz), None, k_row_first * hx]
        if step < LAST:
            for c in range(6):
                set_e(run, c, CX - 1, e_rows(run, c, CX - 1) + plane_last[c])
            for c in range(6):
                if plane_first[c] is not None:
                    set_e(run, c, 0, e_rows(run, c, 0) + plane_first[c])
            for c in range(6):
                efield[run, c, E_LAST, :] = efield[run, c, E_LAST, :] + row_last[c]
            for c in range(6):
                if row_first[c] is not None:
                    efield[run, c, E_FIRST, :] = efield[run, c, E_FIRST, :] + row_first[c]
        else:
            out = outs[run]
            for rows, gains in (
                (slice(CY * (CX - 1), CY * CX), plane_last),
                (slice(0, CY), plane_first),
                (FINAL, row_last),
                (FIRST, row_first),
            ):
                for c in range(3):
                    if gains[c] is not None:
                        real, imag = rotate((gains[c], gains[3 + c]), *turn(step))
                        out[0, c, rows, :] = out[0, c, rows, :] + real
                        out[0, 3 + c, rows, :] = out[0, 3 + c, rows, :] + imag

    def term(rows):
        total = None
        for c in range(3):
            value = ft[0, c, rows, :] * at[0, c, rows, :] - ft[0, 3 + c, rows, :] * at[0, 3 + c, rows, :]
            total = value if total is None else total + value
        return total

    for run in range(2):
        for copy in field_loads[run]:
            copy.wait()
        stage_e(0, run)
        stage_h(0, run)
        if run == 0:
            pl.semaphore_wait(barrier, len(DIRECT) + n_a - 1)
        for kind in DIRECT:
            make(0, run, kind).start()
    for kind in (EY_MSG, PY_MSG):
        pl.semaphore_signal(ready_sem, inc=1, device_id=shifted(kind), device_id_type=MESH)
    perm_load.wait()
    for x in range(CX):
        coef[x] = COURANT / coef[x]
    bulk(0, 0)
    pl.semaphore_wait(ready_sem, 2)
    for run in range(2):
        for kind in CORNERS:
            make(0, run, kind).start()
    bulk(0, 1)
    for copy in spec_loads:
        copy.wait()

    for step in range(STEPS):
        for run in range(2):
            receive(step, run)
            arrive(step, run)
            if step < LAST:
                stage_e(step + 1, run)
                for kind in (CORNER_A, CORNER_B, EY_MSG, EX_MSG):
                    make(step + 1, run, kind).start()
                stage_h(step + 1, run)
                for kind in (PY_MSG, PX_MSG):
                    make(step + 1, run, kind).start()
        if step < LAST:
            for run in range(2):
                bulk(step + 1, run)
        if step == LAST - 1:
            for x in range(1, CX - 1):
                terms[x] = term(slice(CY * x, CY * (x + 1)))

    flat = terms.reshape(CX * CY, NZ)
    flat[FIRST, :] = term(FIRST)
    flat[FINAL, :] = term(FINAL)
    block = lane // CHUNK
    planes = [term(slice(CY * x, CY * (x + 1))) if x in (0, CX - 1) else terms[x] for x in range(CX)]
    for stride in (1, 2, 4):
        low = (block // stride) % 2 == 0
        fresh = list(planes)
        for j in range(GROUPS):
            if (j // stride) % 2 == 0:
                a, b = planes[j], planes[j + stride]
                fresh[j] = jnp.where(low, a, pltpu.roll(b, CHUNK * stride, 1))
                fresh[j + stride] = jnp.where(low, pltpu.roll(a, NZ - CHUNK * stride, 1), b)
        planes = fresh
    for j in range(GROUPS):
        packed[j] = planes[j]

    def share(offset):
        peer = angle_peer(offset)
        return pltpu.make_async_remote_copy(
            src_ref=packed.at[peer["angle"]],
            dst_ref=landed.at[offset],
            send_sem=gsend_sem.at[offset],
            recv_sem=grecv_sem.at[offset],
            device_id=peer,
            device_id_type=MESH,
        )

    for offset in (4, 3, 5, 2, 6, 1, 7):
        share(offset).start()
    for step in range(STEPS):
        for run in range(2):
            for kind in range(6):
                make(step, run, kind).wait_send()
    own_tile = me_x * n_y + me_y
    hits = jnp.int32(0)
    for i in range(tiles.shape[0]):
        hits = hits + jnp.where(tiles[i] == own_tile, 1, 0)
    chosen = jnp.full((CY, NZ), hits, jnp.int32) > 0
    total = packed[me_a]
    for offset in range(1, n_a):
        share(offset).wait_recv()
        total = total + landed[offset]
    total = jnp.where(chosen, total * (1.0 / GROUPS), 0.0)
    for j in range(CX):
        moved = total if j == 0 else pltpu.roll(total, NZ - CHUNK * j, 1)
        grad[j] = moved[:, 0:CHUNK]
    for offset in range(1, n_a):
        share(offset).wait_send()


def write_out(ft, at, grad, ft_out, at_out, grad_out, sem):
    copies = [
        pltpu.make_async_copy(src, dst, sem.at[i])
        for i, (src, dst) in enumerate(((ft, ft_out), (at, at_out), (grad, grad_out)))
    ]
    for copy in copies:
        copy.start()
    for copy in copies:
        copy.wait()


def shards(ff, af, fs, as_, perm, phase_table, angle_index, design_tiles):
    f32 = jnp.float32
    hbm = pl.BlockSpec(memory_space=pl.ANY)
    vmem = pl.BlockSpec(memory_space=pltpu.VMEM)
    loads = 2 * 2 * CX + 6
    flat = (1, 6, CX * CY, NZ)
    cells = (1, 6, CX, CY, NZ)
    held = pl.pallas_call(
        kernel,
        out_shape=(pltpu.VMEM(flat, f32), pltpu.VMEM(flat, f32), pltpu.VMEM((CX, CY, CHUNK), f32)),
        in_specs=[hbm] * 8,
        out_specs=(vmem, vmem, vmem),
        scratch_shapes=[
            pltpu.VMEM((2, 6, (CX + 1) * ROWS, NZ), f32),
            pltpu.VMEM((2, 6, (CX + 1) * ROWS, NZ), f32),
            pltpu.VMEM((CX, CY, NZ), f32),
            pltpu.VMEM((8, 8, NZ), f32),
            pltpu.VMEM((CX, CY, NZ), f32),
            pltpu.VMEM((GROUPS, CY, NZ), f32),
            pltpu.VMEM((GROUPS, CY, NZ), f32),
            pltpu.VMEM((STEPS, 2, 2, 4, CY, NZ), f32),
            pltpu.VMEM((STEPS, 2, 2, 4, CX, NZ), f32),
            pltpu.VMEM((STEPS, 2, 2, 2, NZ), f32),
            pltpu.VMEM((STEPS, 2, 2, 4, CY, NZ), f32),
            pltpu.VMEM((STEPS, 2, 2, 4, CX, NZ), f32),
            pltpu.VMEM((STEPS, 2, 2, 2, NZ), f32),
            pltpu.SMEM((2, GROUPS), f32),
            pltpu.SMEM((1,), jnp.int32),
            pltpu.SMEM(design_tiles.shape, jnp.int32),
            pltpu.SemaphoreType.DMA((loads,)),
            pltpu.SemaphoreType.DMA((STEPS, 2, 6)),
            pltpu.SemaphoreType.DMA((STEPS, 2, 6)),
            pltpu.SemaphoreType.DMA((GROUPS,)),
            pltpu.SemaphoreType.DMA((GROUPS,)),
            pltpu.SemaphoreType.REGULAR,
        ],
        compiler_params=pltpu.CompilerParams(collective_id=0, has_side_effects=True),
        name="fdtd",
    )(ff, af, fs.reshape(flat), as_.reshape(flat), perm, phase_table.T, angle_index, design_tiles)
    ft, at, grad = pl.pallas_call(
        write_out,
        out_shape=(
            jax.ShapeDtypeStruct(flat, f32),
            jax.ShapeDtypeStruct(flat, f32),
            jax.ShapeDtypeStruct((CX, CY, CHUNK), f32),
        ),
        in_specs=[hbm] * 3,
        out_specs=(hbm,) * 3,
        scratch_shapes=[pltpu.SemaphoreType.DMA((3,))],
        name="write_out",
    )(*(pltpu.with_memory_space_constraint(a, pltpu.VMEM) for a in held))
    return ft.reshape(cells), at.reshape(cells), grad


def solution(mesh):
    in_specs = (
        P("angle", None, "gx", "gy", None),
        P("angle", None, "gx", "gy", None),
        P("angle", None, "gx", "gy", None),
        P("angle", None, "gx", "gy", None),
        P("gx", "gy", None),
        P(),
        P("angle"),
        P(),
    )
    out_specs = (
        P("angle", None, "gx", "gy", None),
        P("angle", None, "gx", "gy", None),
        P("gx", "gy", "angle"),
    )
    return jax.shard_map(shards, mesh=mesh, in_specs=in_specs, out_specs=out_specs, check_vma=False)
```

```python
import math

import jax
import jax.numpy as jnp
from jax import lax
from jax.experimental import pallas as pl
from jax.experimental.pallas import tpu as pltpu
from jax.sharding import PartitionSpec as P

STEPS = 3
COURANT = 0.5
OMEGA_STEP = 0.7
CX, CY, NZ = 8, 16, 128
ROWS = 24
GROUPS = 8
CHUNK = NZ // GROUPS
MESH = pl.DeviceIdType.MESH
LAST = STEPS - 1

KINDS = ((1, -1), (-1, 1), (-1, 0), (1, 0), (0, -1), (0, 1))
CORNER_A, CORNER_B, EX_MSG, PX_MSG, EY_MSG, PY_MSG = range(6)
DIRECT = (EY_MSG, PY_MSG, EX_MSG, PX_MSG)
CORNERS = (CORNER_A, CORNER_B)

E_FIRST = pl.ds(0, CX, stride=ROWS)
E_LAST = pl.ds(CY - 1, CX, stride=ROWS)
E_LAST_NEXT_X = pl.ds(ROWS + CY - 1, CX, stride=ROWS)
H_LAST = pl.ds(ROWS + 8 + CY - 1, CX, stride=ROWS)
FIRST = pl.ds(0, CX, stride=CY)
FINAL = pl.ds(CY - 1, CX, stride=CY)


def rotate(pair, cosine, sine):
    real_part, imag_part = pair
    return real_part * cosine - imag_part * sine, real_part * sine + imag_part * cosine


def kernel(
    ff, af, fs, as_, perm, phase_in, aidx_in, tiles_in,
    ft, at, grad,
    efield, hfield, coef, phs, terms, packed, landed,
    sx, sy, sc, rx, ry, rc,
    phase, aidx, tiles,
    load_sem, send_sem, recv_sem, gsend_sem, grecv_sem, ready_sem,
):
    me_a = lax.axis_index("angle")
    me_x = lax.axis_index("gx")
    me_y = lax.axis_index("gy")
    n_a, n_x, n_y = GROUPS, lax.axis_size("gx"), lax.axis_size("gy")

    def shifted(kind):
        dx, dy = KINDS[kind]
        return {"gx": lax.rem(me_x + dx + n_x, n_x), "gy": lax.rem(me_y + dy + n_y, n_y)}

    def angle_peer(offset):
        return {"angle": lax.rem(me_a + offset, n_a)}

    barrier = pltpu.get_barrier_semaphore()
    for kind in DIRECT:
        pl.semaphore_signal(barrier, inc=1, device_id=shifted(kind), device_id_type=MESH)
    for offset in range(1, n_a):
        pl.semaphore_signal(barrier, inc=1, device_id=angle_peer(offset), device_id_type=MESH)

    count = [0]

    def load(src, dst):
        copy = pltpu.make_async_copy(src, dst, load_sem.at[count[0]])
        count[0] += 1
        copy.start()
        return copy

    small_loads = [load(aidx_in, aidx), load(phase_in, phase), load(tiles_in, tiles)]
    field_loads = []
    for run, src in enumerate((ff, af)):
        group = []
        for x in range(CX):
            group.append(load(src.at[0, 0:6, x], efield.at[run, :, ROWS * x : ROWS * x + CY, :]))
            base = ROWS * (x + 1) + 8
            group.append(load(src.at[0, 6:12, x], hfield.at[run, :, base : base + CY, :]))
        field_loads.append(group)
    perm_load = load(perm, coef)
    spec_loads = [load(fs, ft), load(as_, at)]

    zero_rows = jnp.zeros((8, NZ), jnp.float32)
    zero_plane = jnp.zeros((CY, NZ), jnp.float32)
    for run in range(2):
        for c in range(6):
            for x in range(CX):
                efield[run, c, ROWS * x + CY : ROWS * (x + 1), :] = zero_rows
                hfield[run, c, ROWS * (x + 1) : ROWS * (x + 1) + 8, :] = zero_rows
            efield[run, c, ROWS * CX : ROWS * CX + CY, :] = zero_plane
            hfield[run, c, 8 : 8 + CY, :] = zero_plane

    lane = lax.broadcasted_iota(jnp.int32, (CY, NZ), 1)
    not_last = lane < NZ - 1
    not_first = lane > 0
    row_index = lax.broadcasted_iota(jnp.int32, (CY, NZ), 0)
    x_index = lax.broadcasted_iota(jnp.int32, (CX, NZ), 0)

    def phase_pair(which, run, rows):
        c = phs[2 * which, 0:1, :]
        s = phs[2 * which + 1, 0:1, :]
        s = s if run == 0 else -s
        return jnp.broadcast_to(c, (rows, NZ)), jnp.broadcast_to(s, (rows, NZ))

    def e_rows(run, c, x, start=0):
        return efield[run, c, ROWS * x + start : ROWS * x + start + CY, :]

    def set_e(run, c, x, value):
        efield[run, c, ROWS * x : ROWS * x + CY, :] = value

    def h_rows(run, c, x, start=0):
        base = ROWS * (x + 1) + 8 + start
        return hfield[run, c, base : base + CY, :]

    def set_h(run, c, x, value):
        base = ROWS * (x + 1) + 8
        hfield[run, c, base : base + CY, :] = value

    def next_z(value):
        return jnp.where(not_last[: value.shape[0]], pltpu.roll(value, NZ - 1, 1), 0.0)

    def prev_z(value):
        return jnp.where(not_first[: value.shape[0]], pltpu.roll(value, 1, 1), 0.0)

    def make(step, run, kind):
        if kind in CORNERS:
            src, dst = sc.at[step, run, kind], rc.at[step, run, kind]
        elif kind in (EX_MSG, PX_MSG):
            src, dst = sx.at[step, run, kind - EX_MSG], rx.at[step, run, kind - EX_MSG]
        else:
            src, dst = sy.at[step, run, kind - EY_MSG], ry.at[step, run, kind - EY_MSG]
        return pltpu.make_async_remote_copy(
            src_ref=src,
            dst_ref=dst,
            send_sem=send_sem.at[step, run, kind],
            recv_sem=recv_sem.at[step, run, kind],
            device_id=shifted(kind),
            device_id_type=MESH,
        )

    def stage_e(step, run):
        for part in range(2):
            b = 3 * part
            sc[step, run, CORNER_A, part : part + 1, :] = efield[run, b, ROWS * 7 : ROWS * 7 + 1, :]
            sc[step, run, CORNER_B, part : part + 1, :] = efield[run, b + 1, CY - 1 : CY, :]
            for slot, c in enumerate((1, 2)):
                sx[step, run, 0, 2 * part + slot] = e_rows(run, b + c, 0)
            for slot, c in enumerate((0, 2)):
                sy[step, run, 0, 2 * part + slot] = efield[run, b + c, E_FIRST, :]

    def h_value(run, part, x):
        b = 3 * part
        ex, ey, ez = (e_rows(run, b + c, x) for c in range(3))
        dz_dy = e_rows(run, b + 2, x, 1) - ez
        dx_dy = e_rows(run, b, x, 1) - ex
        dy_dz = next_z(ey) - ey
        dx_dz = next_z(ex) - ex
        dz_dx = e_rows(run, b + 2, x + 1) - ez
        dy_dx = e_rows(run, b + 1, x + 1) - ey
        hx = h_rows(run, b, x) - COURANT * (dz_dy - dy_dz)
        hy = h_rows(run, b + 1, x) - COURANT * (dx_dz - dz_dx)
        hz = h_rows(run, b + 2, x) - COURANT * (dy_dx - dx_dy)
        return hx, hy, hz

    def stage_h(step, run):
        for part in range(2):
            b = 3 * part
            ex, ey, ez = (efield[run, b + c, E_LAST, :] for c in range(3))
            ey_next = efield[run, b + 1, E_LAST_NEXT_X, :]
            hx = hfield[run, b, H_LAST, :] + COURANT * (ez + (next_z(ey) - ey))
            hz = hfield[run, b + 2, H_LAST, :] - COURANT * ((ey_next - ey) + ex)
            sy[step, run, 1, 2 * part] = hx
            sy[step, run, 1, 2 * part + 1] = hz
        for part in range(2):
            b = 3 * part
            hx, hy, hz = h_value(run, part, CX - 1)
            sx[step, run, 1, 2 * part] = hy
            sx[step, run, 1, 2 * part + 1] = hz
            for c, value in enumerate((hx, hy, hz)):
                set_h(run, b + c, CX - 1, value)

    outs = (ft, at)

    def turn(step):
        theta = OMEGA_STEP * (step + 1)
        return math.cos(theta), math.sin(theta)

    def bulk(step, run):
        for x in range(CX - 1):
            for part in range(2):
                for c, value in enumerate(h_value(run, part, x)):
                    set_h(run, 3 * part + c, x, value)
        out = outs[run]
        for x in range(CX):
            k = coef[x]
            old, new = [], []
            for part in range(2):
                b = 3 * part
                hx, hy, hz = (h_rows(run, b + c, x) for c in range(3))
                curl_x = (hz - h_rows(run, b + 2, x, -1)) - (hy - prev_z(hy))
                curl_y = (hx - prev_z(hx)) - (hz - h_rows(run, b + 2, x - 1))
                curl_z = (hy - h_rows(run, b + 1, x - 1)) - (hx - h_rows(run, b, x, -1))
                for c, curl in enumerate((curl_x, curl_y, curl_z)):
                    e = e_rows(run, b + c, x)
                    old.append(e)
                    new.append(e + k * curl)
            rows = slice(CY * x, CY * (x + 1))
            for c in range(3):
                real, imag = None, None
                if step > 0:
                    real, imag = rotate((old[c], old[3 + c]), *turn(step - 1))
                if step == LAST:
                    more = rotate((new[c], new[3 + c]), *turn(step))
                    real = more[0] if real is None else real + more[0]
                    imag = more[1] if imag is None else imag + more[1]
                if real is not None:
                    out[0, c, rows, :] = out[0, c, rows, :] + real
                    out[0, 3 + c, rows, :] = out[0, 3 + c, rows, :] + imag
            if step < LAST:
                for c in range(6):
                    set_e(run, c, x, new[c])

    def receive(step, run):
        for kind in range(6):
            make(step, run, kind).wait_recv()

    def arrive(step, run):
        fwd_x, fwd_y = phase_pair(0, run, CY), phase_pair(2, run, CX)
        back_x, back_y = phase_pair(1, run, CY), phase_pair(3, run, CX)
        one_x, one_y = phase_pair(0, run, 1), phase_pair(2, run, 1)
        eyx = rotate((rx[step, run, 0, 0], rx[step, run, 0, 2]), *fwd_x)
        ezx = rotate((rx[step, run, 0, 1], rx[step, run, 0, 3]), *fwd_x)
        exy = rotate((ry[step, run, 0, 0], ry[step, run, 0, 2]), *fwd_y)
        ezy = rotate((ry[step, run, 0, 1], ry[step, run, 0, 3]), *fwd_y)
        corner_a = rotate((rc[step, run, CORNER_A, 0:1, :], rc[step, run, CORNER_A, 1:2, :]), *one_y)
        corner_b = rotate((rc[step, run, CORNER_B, 0:1, :], rc[step, run, CORNER_B, 1:2, :]), *one_x)
        pz = tuple(
            rx[step, run, 1, 2 * part + 1]
            + jnp.where(row_index == CY - 1, jnp.broadcast_to(COURANT * corner_a[part], (CY, NZ)), 0.0)
            for part in range(2)
        )
        qz = tuple(
            ry[step, run, 1, 2 * part + 1]
            - jnp.where(x_index == CX - 1, jnp.broadcast_to(COURANT * corner_b[part], (CX, NZ)), 0.0)
            for part in range(2)
        )
        hy_x = rotate((rx[step, run, 1, 0], rx[step, run, 1, 2]), *back_x)
        hz_x = rotate(pz, *back_x)
        hx_y = rotate((ry[step, run, 1, 0], ry[step, run, 1, 2]), *back_y)
        hz_y = rotate(qz, *back_y)
        k_first, k_last = coef[0], coef[CX - 1]
        k_row_first, k_row_last = coef.reshape(CX * CY, NZ)[FIRST, :], coef.reshape(CX * CY, NZ)[FINAL, :]
        plane_last, row_last, plane_first, row_first = [], [], [], []
        for part in range(2):
            b = 3 * part
            dy_plane, dz_plane = COURANT * ezx[part], -COURANT * eyx[part]
            dx_row, dz_row = -COURANT * ezy[part], COURANT * exy[part]
            if step < LAST:
                set_h(run, b + 1, CX - 1, h_rows(run, b + 1, CX - 1) + dy_plane)
                set_h(run, b + 2, CX - 1, h_rows(run, b + 2, CX - 1) + dz_plane)
                hfield[run, b, H_LAST, :] = hfield[run, b, H_LAST, :] + dx_row
                hfield[run, b + 2, H_LAST, :] = hfield[run, b + 2, H_LAST, :] + dz_row
            dz_above = jnp.where(row_index > 0, pltpu.roll(dz_plane, 1, 0), 0.0)
            dz_before = jnp.where(x_index > 0, pltpu.roll(dz_row, 1, 0), 0.0)
            plane_last += [
                k_last * ((dz_plane - dz_above) - (dy_plane - prev_z(dy_plane))),
                -(k_last * dz_plane),
                k_last * dy_plane,
            ]
            row_last += [
                k_row_last * dz_row,
                k_row_last * ((dx_row - prev_z(dx_row)) - (dz_row - dz_before)),
                -(k_row_last * dx_row),
            ]
            hy = hy_x[part] + COURANT * sx[step, run, 0, 2 * part + 1]
            hz = hz_x[part] - COURANT * sx[step, run, 0, 2 * part]
            plane_first += [None, k_first * hz, -(k_first * hy)]
            hx = hx_y[part] - COURANT * sy[step, run, 0, 2 * part + 1]
            hz = hz_y[part] + COURANT * sy[step, run, 0, 2 * part]
            row_first += [-(k_row_first * hz), None, k_row_first * hx]
        if step < LAST:
            for c in range(6):
                set_e(run, c, CX - 1, e_rows(run, c, CX - 1) + plane_last[c])
            for c in range(6):
                if plane_first[c] is not None:
                    set_e(run, c, 0, e_rows(run, c, 0) + plane_first[c])
            for c in range(6):
                efield[run, c, E_LAST, :] = efield[run, c, E_LAST, :] + row_last[c]
            for c in range(6):
                if row_first[c] is not None:
                    efield[run, c, E_FIRST, :] = efield[run, c, E_FIRST, :] + row_first[c]
        else:
            out = outs[run]
            for rows, gains in (
                (slice(CY * (CX - 1), CY * CX), plane_last),
                (slice(0, CY), plane_first),
                (FINAL, row_last),
                (FIRST, row_first),
            ):
                for c in range(3):
                    if gains[c] is not None:
                        real, imag = rotate((gains[c], gains[3 + c]), *turn(step))
                        out[0, c, rows, :] = out[0, c, rows, :] + real
                        out[0, 3 + c, rows, :] = out[0, 3 + c, rows, :] + imag

    def term(rows):
        total = None
        for c in range(3):
            value = ft[0, c, rows, :] * at[0, c, rows, :] - ft[0, 3 + c, rows, :] * at[0, 3 + c, rows, :]
            total = value if total is None else total + value
        return total

    for run in range(2):
        for copy in field_loads[run]:
            copy.wait()
        stage_e(0, run)
        stage_h(0, run)
        if run == 0:
            pl.semaphore_wait(barrier, len(DIRECT) + n_a - 1)
        for kind in DIRECT:
            make(0, run, kind).start()
    for kind in (EY_MSG, PY_MSG):
        pl.semaphore_signal(ready_sem, inc=1, device_id=shifted(kind), device_id_type=MESH)

    for copy in small_loads:
        copy.wait()
    row = aidx[0]
    for axis, (place, last) in enumerate(((me_x, n_x - 1), (me_y, n_y - 1))):
        angle = jnp.full((8, NZ), phase[axis, row], jnp.float32)
        cosine, sine = jnp.cos(angle), jnp.sin(angle)
        one, zero = jnp.ones_like(cosine), jnp.zeros_like(cosine)
        ahead = jnp.full((8, NZ), place, jnp.int32) == last
        behind = jnp.full((8, NZ), place, jnp.int32) == 0
        phs[4 * axis] = jnp.where(ahead, cosine, one)
        phs[4 * axis + 1] = jnp.where(ahead, sine, zero)
        phs[4 * axis + 2] = jnp.where(behind, cosine, one)
        phs[4 * axis + 3] = jnp.where(behind, -sine, zero)

    perm_load.wait()
    for x in range(CX):
        coef[x] = COURANT / coef[x]
    bulk(0, 0)
    pl.semaphore_wait(ready_sem, 2)
    for run in range(2):
        for kind in CORNERS:
            make(0, run, kind).start()
    bulk(0, 1)
    for copy in spec_loads:
        copy.wait()

    for step in range(STEPS):
        for run in range(2):
            receive(step, run)
            arrive(step, run)
            if step < LAST:
                stage_e(step + 1, run)
                for kind in (EY_MSG, CORNER_A, CORNER_B, EX_MSG):
                    make(step + 1, run, kind).start()
                stage_h(step + 1, run)
                for kind in (PY_MSG, PX_MSG):
                    make(step + 1, run, kind).start()
        if step < LAST:
            for run in range(2):
                bulk(step + 1, run)
        if step == LAST - 1:
            for x in range(1, CX - 1):
                terms[x] = term(slice(CY * x, CY * (x + 1)))

    flat = terms.reshape(CX * CY, NZ)
    flat[FIRST, :] = term(FIRST)
    flat[FINAL, :] = term(FINAL)
    block = lane // CHUNK
    planes = [term(slice(CY * x, CY * (x + 1))) if x in (0, CX - 1) else terms[x] for x in range(CX)]
    for stride in (1, 2, 4):
        low = (block // stride) % 2 == 0
        fresh = list(planes)
        for j in range(GROUPS):
            if (j // stride) % 2 == 0:
                a, b = planes[j], planes[j + stride]
                fresh[j] = jnp.where(low, a, pltpu.roll(b, CHUNK * stride, 1))
                fresh[j + stride] = jnp.where(low, pltpu.roll(a, NZ - CHUNK * stride, 1), b)
        planes = fresh
    for j in range(GROUPS):
        packed[j] = planes[j]

    def share(offset):
        peer = angle_peer(offset)
        return pltpu.make_async_remote_copy(
            src_ref=packed.at[peer["angle"]],
            dst_ref=landed.at[offset],
            send_sem=gsend_sem.at[offset],
            recv_sem=grecv_sem.at[offset],
            device_id=peer,
            device_id_type=MESH,
        )

    for offset in (4, 3, 5, 2, 6, 1, 7):
        share(offset).start()
    for step in range(STEPS):
        for run in range(2):
            for kind in range(6):
                make(step, run, kind).wait_send()
    own_tile = me_x * n_y + me_y
    hits = jnp.int32(0)
    for i in range(tiles.shape[0]):
        hits = hits + jnp.where(tiles[i] == own_tile, 1, 0)
    chosen = jnp.full((CY, NZ), hits, jnp.int32) > 0
    total = packed[me_a]
    for offset in range(1, n_a):
        share(offset).wait_recv()
        total = total + landed[offset]
    total = jnp.where(chosen, total * (1.0 / GROUPS), 0.0)
    for j in range(CX):
        moved = total if j == 0 else pltpu.roll(total, NZ - CHUNK * j, 1)
        grad[j] = moved[:, 0:CHUNK]
    for offset in range(1, n_a):
        share(offset).wait_send()


def write_out(ft, at, grad, ft_out, at_out, grad_out, sem):
    copies = [
        pltpu.make_async_copy(src, dst, sem.at[i])
        for i, (src, dst) in enumerate(((ft, ft_out), (at, at_out), (grad, grad_out)))
    ]
    for copy in copies:
        copy.start()
    for copy in copies:
        copy.wait()


def shards(ff, af, fs, as_, perm, phase_table, angle_index, design_tiles):
    f32 = jnp.float32
    hbm = pl.BlockSpec(memory_space=pl.ANY)
    vmem = pl.BlockSpec(memory_space=pltpu.VMEM)
    loads = 2 * 2 * CX + 6
    flat = (1, 6, CX * CY, NZ)
    cells = (1, 6, CX, CY, NZ)
    held = pl.pallas_call(
        kernel,
        out_shape=(pltpu.VMEM(flat, f32), pltpu.VMEM(flat, f32), pltpu.VMEM((CX, CY, CHUNK), f32)),
        in_specs=[hbm] * 8,
        out_specs=(vmem, vmem, vmem),
        scratch_shapes=[
            pltpu.VMEM((2, 6, (CX + 1) * ROWS, NZ), f32),
            pltpu.VMEM((2, 6, (CX + 1) * ROWS, NZ), f32),
            pltpu.VMEM((CX, CY, NZ), f32),
            pltpu.VMEM((8, 8, NZ), f32),
            pltpu.VMEM((CX, CY, NZ), f32),
            pltpu.VMEM((GROUPS, CY, NZ), f32),
            pltpu.VMEM((GROUPS, CY, NZ), f32),
            pltpu.VMEM((STEPS, 2, 2, 4, CY, NZ), f32),
            pltpu.VMEM((STEPS, 2, 2, 4, CX, NZ), f32),
            pltpu.VMEM((STEPS, 2, 2, 2, NZ), f32),
            pltpu.VMEM((STEPS, 2, 2, 4, CY, NZ), f32),
            pltpu.VMEM((STEPS, 2, 2, 4, CX, NZ), f32),
            pltpu.VMEM((STEPS, 2, 2, 2, NZ), f32),
            pltpu.SMEM((2, GROUPS), f32),
            pltpu.SMEM((1,), jnp.int32),
            pltpu.SMEM(design_tiles.shape, jnp.int32),
            pltpu.SemaphoreType.DMA((loads,)),
            pltpu.SemaphoreType.DMA((STEPS, 2, 6)),
            pltpu.SemaphoreType.DMA((STEPS, 2, 6)),
            pltpu.SemaphoreType.DMA((GROUPS,)),
            pltpu.SemaphoreType.DMA((GROUPS,)),
            pltpu.SemaphoreType.REGULAR,
        ],
        compiler_params=pltpu.CompilerParams(collective_id=0, has_side_effects=True),
        name="fdtd",
    )(ff, af, fs.reshape(flat), as_.reshape(flat), perm, phase_table.T, angle_index, design_tiles)
    ft, at, grad = pl.pallas_call(
        write_out,
        out_shape=(
            jax.ShapeDtypeStruct(flat, f32),
            jax.ShapeDtypeStruct(flat, f32),
            jax.ShapeDtypeStruct((CX, CY, CHUNK), f32),
        ),
        in_specs=[hbm] * 3,
        out_specs=(hbm,) * 3,
        scratch_shapes=[pltpu.SemaphoreType.DMA((3,))],
        name="write_out",
    )(*(pltpu.with_memory_space_constraint(a, pltpu.VMEM) for a in held))
    return ft.reshape(cells), at.reshape(cells), grad


def solution(mesh):
    in_specs = (
        P("angle", None, "gx", "gy", None),
        P("angle", None, "gx", "gy", None),
        P("angle", None, "gx", "gy", None),
        P("angle", None, "gx", "gy", None),
        P("gx", "gy", None),
        P(),
        P("angle"),
        P(),
    )
    out_specs = (
        P("angle", None, "gx", "gy", None),
        P("angle", None, "gx", "gy", None),
        P("gx", "gy", "angle"),
    )
    return jax.shard_map(shards, mesh=mesh, in_specs=in_specs, out_specs=out_specs, check_vma=False)
```
